32 devices in a mesh: cuts: 2 (over x), brick: 16 (over z, y, core).
Axes of the slice: x: 2, y: 2, z: 4, core: 2. Of those that a mesh axis runs over, the one named last changes fastest.
Arguments:
- eigen_vectors: float32 [64, 2, 3, 64, 512], P(None, None, None, ('cuts', 'brick')), parts along dimension 3, may hold values from -6 to 6
- link_field: float32 [3, 2, 3, 3, 64, 512], P(None, None, None, None, ('cuts', 'brick')), parts along dimension 4, may hold values from -3 to 3
- block_slot: int32 [63], replicated, may hold values from 0 to 63, as said below
Outputs:
- elementals: float32 [128, 32, 128], P(('cuts', 'brick')), parts along dimension 0
The draws below stay inside these ranges and needn't reach their ends.
There are 2 independent parts, one for each index of `cuts`. The reference program is written for one: setup_inputs(seed, part) draws one part's arguments, and reference() takes and returns one part's arrays. A program takes and returns all parts, laid end to end along the dimension named above; an argument that names none is the same for every part. Nothing has to cross between parts.
Inputs may be any that keep to these rules, and one draw needn't show every extreme that they name: block_slot names distinct slots; slot s belongs to device s // 4 of the brick axis; in every draw some device has all 4 of its slots named.
All inputs are finite; a program needn't handle non-finite values.
Results may differ from the reference program's by a relative error of at most 0.0044.
Values sent between devices are 32-bit elements; how exact they have to be, the bound alone decides.
A program may use at most 64 MiB of HBM per device.

```python
import math
import jax
import jax.numpy as jnp
import numpy as np
from jax import lax

NV = 64
PB = 32
CAP = 4
LX = 8
LY = 64
LZ = 32
NBLK = 63
SLOTS = 64


def draw_block_slot(key, part):
    key_owner, key_score, key_order = jax.random.split(key, 3)
    slot_ids = jnp.arange(SLOTS, dtype=jnp.int32)
    full_owner = jax.random.randint(key_owner, (), 0, SLOTS // CAP)
    slot_score = jax.random.permutation(key_score, SLOTS).astype(jnp.int32)
    slot_score = jnp.where(slot_ids // CAP == full_owner, slot_ids % CAP - CAP, slot_score)
    slot_order = jnp.argsort(slot_score, stable=True)[:NBLK]
    return jax.random.permutation(key_order, slot_order).astype(jnp.int32)


def block_scale(own_key, shape, cuts, low, high):
    level, own = 1.0, jax.random.fold_in(own_key, 6)
    for axis_at, shards_of in cuts:
        draws = jnp.exp(jax.random.uniform(jax.random.fold_in(own, axis_at), (shards_of,), jnp.float32, low / len(cuts), high / len(cuts)))
        level = level * jnp.repeat(draws, shape[axis_at] // shards_of).reshape([-1 if axis == axis_at else 1 for axis in range(len(shape))])
    return level


def centred(rng, shape, spread, limit, cuts=(), kind=jnp.bfloat16):
    array = jax.random.normal(rng, shape, jnp.float32) * spread
    if len(cuts) > 0:
        array = block_scale(rng, shape, cuts, -0.22, 0.18) * array
    return jnp.clip(array, min=-limit, max=limit).astype(kind)


def setup_inputs(seed: int = 0, part: int = 0) -> dict:
    splits = jax.random.split(jax.random.key(seed), 4)
    own_keys = jax.random.split(jax.random.fold_in(splits[3], part), 4)
    eigen_vectors = centred(own_keys[0], (NV, 2, 3, LZ, LX * LY), 1.0, 6.0, ((3, 16),), jnp.float32)
    link_field = centred(own_keys[1], (3, 2, 3, 3, LZ, LX * LY), 0.5, 3.0, ((4, 16),), jnp.float32)
    block_slot = draw_block_slot(jax.random.fold_in(splits[3], 71), part)
    return dict(eigen_vectors=eigen_vectors, link_field=link_field, block_slot=block_slot)


def periodic(lattice_field, rim_depth, along):
    plane_count = lattice_field.shape[along]
    lower = lax.slice_in_dim(lattice_field, plane_count - rim_depth, plane_count, axis=along)
    upper = lax.slice_in_dim(lattice_field, 0, rim_depth, axis=along)
    return jnp.concatenate([lower, lattice_field, upper], axis=along)

def shift_columns(lattice_field, forward):
    column = jnp.arange(lattice_field.shape[-1]) % LX
    if forward:
        return jnp.where(column == LX - 1, jnp.roll(lattice_field, LX - 1, axis=-1), jnp.roll(lattice_field, -1, axis=-1))
    return jnp.where(column == 0, jnp.roll(lattice_field, -(LX - 1), axis=-1), jnp.roll(lattice_field, 1, axis=-1))

def link_times(link_set, lattice_field):
    real_rows = []
    imag_rows = []
    for out_row in range(3):
        real_part = link_set[0, out_row, 0] * lattice_field[:, 0, 0] - link_set[1, out_row, 0] * lattice_field[:, 1, 0]
        imag_part = link_set[0, out_row, 0] * lattice_field[:, 1, 0] + link_set[1, out_row, 0] * lattice_field[:, 0, 0]
        for in_row in (1, 2):
            real_part = real_part + link_set[0, out_row, in_row] * lattice_field[:, 0, in_row] - link_set[1, out_row, in_row] * lattice_field[:, 1, in_row]
            imag_part = imag_part + link_set[0, out_row, in_row] * lattice_field[:, 1, in_row] + link_set[1, out_row, in_row] * lattice_field[:, 0, in_row]
        real_rows.append(real_part)
        imag_rows.append(imag_part)
    return jnp.stack([jnp.stack(real_rows, 1), jnp.stack(imag_rows, 1)], 1)

def adjoint_times(link_set, lattice_field):
    real_rows = []
    imag_rows = []
    for out_row in range(3):
        real_part = link_set[0, 0, out_row] * lattice_field[:, 0, 0] + link_set[1, 0, out_row] * lattice_field[:, 1, 0]
        imag_part = link_set[0, 0, out_row] * lattice_field[:, 1, 0] - link_set[1, 0, out_row] * lattice_field[:, 0, 0]
        for in_row in (1, 2):
            real_part = real_part + link_set[0, in_row, out_row] * lattice_field[:, 0, in_row] + link_set[1, in_row, out_row] * lattice_field[:, 1, in_row]
            imag_part = imag_part + link_set[0, in_row, out_row] * lattice_field[:, 1, in_row] - link_set[1, in_row, out_row] * lattice_field[:, 0, in_row]
        real_rows.append(real_part)
        imag_rows.append(imag_part)
    return jnp.stack([jnp.stack(real_rows, 1), jnp.stack(imag_rows, 1)], 1)

def apply_hops(lattice_field, link_field):
    inner_field = lattice_field[:, :, :, 1:-1]
    inner_links = link_field[:, :, :, :, 1:-1]
    hop_total = link_times(inner_links[0], shift_columns(inner_field, True))
    hop_total = hop_total + shift_columns(adjoint_times(inner_links[0], inner_field), False)
    hop_total = hop_total + link_times(inner_links[1], jnp.roll(inner_field, -LX, axis=4))
    hop_total = hop_total + jnp.roll(adjoint_times(inner_links[1], inner_field), LX, axis=4)
    hop_total = hop_total + link_times(link_field[2][:, :, :, 1:-1], lattice_field[:, :, :, 2:])
    hop_total = hop_total + adjoint_times(link_field[2][:, :, :, :-2], lattice_field[:, :, :, :-2])
    return hop_total * (1.0 / 6.0)

def diquark_block(left_rows, right_rows):
    real_rows = []
    imag_rows = []
    for colour in range(3):
        first_colour = (colour + 1) % 3
        second_colour = (colour + 2) % 3
        real_part = left_rows[:, 0, first_colour] * right_rows[:, 0, second_colour] - left_rows[:, 1, first_colour] * right_rows[:, 1, second_colour] - (left_rows[:, 0, second_colour] * right_rows[:, 0, first_colour] - left_rows[:, 1, second_colour] * right_rows[:, 1, first_colour])
        imag_part = left_rows[:, 0, first_colour] * right_rows[:, 1, second_colour] + left_rows[:, 1, first_colour] * right_rows[:, 0, second_colour] - (left_rows[:, 0, second_colour] * right_rows[:, 1, first_colour] + left_rows[:, 1, second_colour] * right_rows[:, 0, first_colour])
        real_rows.append(real_part)
        imag_rows.append(imag_part)
    return jnp.stack([jnp.stack(real_rows, 1), jnp.stack(imag_rows, 1)], 1)

def elemental_block(quarks, vectors_low):
    pair_count = quarks.shape[0]
    vector_count = vectors_low.shape[0]
    left_mat = quarks.astype(jnp.float32).reshape(pair_count * 2, -1)
    right_mat = vectors_low.astype(jnp.float32).reshape(vector_count * 2, -1)
    products = lax.dot_general(left_mat, right_mat, (((1,), (1,)), ((), ())), precision=lax.Precision.HIGHEST, preferred_element_type=jnp.float32)
    products = products.reshape(pair_count, 2, vector_count, 2)
    real_part = products[:, 0, :, 0] - products[:, 1, :, 1]
    imag_part = products[:, 0, :, 1] + products[:, 1, :, 0]
    return jnp.stack([real_part, imag_part], 1).reshape(pair_count, 2 * vector_count)

def reference(eigen_vectors, link_field, block_slot):
    link_wide = periodic(link_field, 1, 4)
    first_step = apply_hops(periodic(eigen_vectors, 1, 3), link_wide)
    filtered = 2.0 * apply_hops(periodic(first_step, 1, 3), link_wide) - eigen_vectors
    vectors_low = filtered.astype(jnp.bfloat16)
    first_index, second_index = np.triu_indices(NV, 1)
    first_table = jnp.asarray(first_index.reshape(NBLK, PB).astype(np.int32))
    second_table = jnp.asarray(second_index.reshape(NBLK, PB).astype(np.int32))

    def one_block(pair_rows):
        quarks = diquark_block(jnp.take(filtered, pair_rows[0], axis=0), jnp.take(filtered, pair_rows[1], axis=0)).astype(jnp.bfloat16)
        return elemental_block(quarks, vectors_low)
    blocks = lax.map(one_block, (first_table, second_table))
    factor = 1.0 / math.sqrt(3.0 * LX * LY * LZ)
    elemental = blocks * factor
    return jnp.zeros((SLOTS, PB, 2 * NV), jnp.float32).at[block_slot].set(elemental)
```

```python
import functools
import math

import jax
import jax.numpy as jnp
from jax import lax
from jax.experimental import pallas as pl
from jax.experimental.pallas import tpu as pltpu
from jax.sharding import PartitionSpec as P

PB = 32
CAP = 4
LX = 8
LY = 64


def padded(cells, sides, width):
    for axis, dim in sides:
        count = lax.axis_size(axis)
        head = lax.slice_in_dim(cells, 0, width, axis=dim)
        tail = lax.slice_in_dim(cells, cells.shape[dim] - width, cells.shape[dim], axis=dim)
        cells = jnp.concatenate(
            [
                lax.ppermute(tail, axis, [(i, (i + 1) % count) for i in range(count)]),
                cells,
                lax.ppermute(head, axis, [((i + 1) % count, i) for i in range(count)]),
            ],
            axis=dim,
        )
    return cells


def from_behind(block, axis, distance):
    devices = range(lax.axis_size(axis))
    route = [((i - distance) % len(devices), i) for i in devices]
    return lax.ppermute(block, axis, route)


def shift_columns(lattice_field, forward):
    column = jnp.arange(lattice_field.shape[-1]) % LX
    if forward:
        return jnp.where(
            column == LX - 1,
            jnp.roll(lattice_field, LX - 1, axis=-1),
            jnp.roll(lattice_field, -1, axis=-1),
        )
    return jnp.where(
        column == 0,
        jnp.roll(lattice_field, -(LX - 1), axis=-1),
        jnp.roll(lattice_field, 1, axis=-1),
    )


def link_times(link_set, lattice_field):
    real_rows = []
    imag_rows = []
    for out_row in range(3):
        real_part = (
            link_set[0, out_row, 0] * lattice_field[:, 0, 0]
            - link_set[1, out_row, 0] * lattice_field[:, 1, 0]
        )
        imag_part = (
            link_set[0, out_row, 0] * lattice_field[:, 1, 0]
            + link_set[1, out_row, 0] * lattice_field[:, 0, 0]
        )
        for in_row in (1, 2):
            real_part = (
                real_part
                + link_set[0, out_row, in_row] * lattice_field[:, 0, in_row]
                - link_set[1, out_row, in_row] * lattice_field[:, 1, in_row]
            )
            imag_part = (
                imag_part
                + link_set[0, out_row, in_row] * lattice_field[:, 1, in_row]
                + link_set[1, out_row, in_row] * lattice_field[:, 0, in_row]
            )
        real_rows.append(real_part)
        imag_rows.append(imag_part)
    return jnp.stack([jnp.stack(real_rows, 1), jnp.stack(imag_rows, 1)], 1)


def adjoint_times(link_set, lattice_field):
    real_rows = []
    imag_rows = []
    for out_row in range(3):
        real_part = (
            link_set[0, 0, out_row] * lattice_field[:, 0, 0]
            + link_set[1, 0, out_row] * lattice_field[:, 1, 0]
        )
        imag_part = (
            link_set[0, 0, out_row] * lattice_field[:, 1, 0]
            - link_set[1, 0, out_row] * lattice_field[:, 0, 0]
        )
        for in_row in (1, 2):
            real_part = (
                real_part
                + link_set[0, in_row, out_row] * lattice_field[:, 0, in_row]
                + link_set[1, in_row, out_row] * lattice_field[:, 1, in_row]
            )
            imag_part = (
                imag_part
                + link_set[0, in_row, out_row] * lattice_field[:, 1, in_row]
                - link_set[1, in_row, out_row] * lattice_field[:, 0, in_row]
            )
        real_rows.append(real_part)
        imag_rows.append(imag_part)
    return jnp.stack([jnp.stack(real_rows, 1), jnp.stack(imag_rows, 1)], 1)


def apply_hops(lattice_field, link_field):
    inner_field = lattice_field[:, :, :, 1:-1]
    inner_links = link_field[:, :, :, :, 1:-1]
    hop_total = link_times(inner_links[0], shift_columns(inner_field, True))
    hop_total = hop_total + shift_columns(adjoint_times(inner_links[0], inner_field), False)
    hop_total = hop_total + link_times(inner_links[1], jnp.roll(inner_field, -LX, axis=4))
    hop_total = hop_total + jnp.roll(adjoint_times(inner_links[1], inner_field), LX, axis=4)
    hop_total = hop_total + link_times(link_field[2][:, :, :, 1:-1], lattice_field[:, :, :, 2:])
    hop_total = hop_total + adjoint_times(link_field[2][:, :, :, :-2], lattice_field[:, :, :, :-2])
    return hop_total * (1.0 / 6.0)


LANES = 128
GROUP = 16
DOT_ROWS = 256


def pair_diquarks(left, right):
    parts = [None] * 6
    for colour in range(3):
        first = (colour + 1) % 3
        second = (colour + 2) % 3
        parts[colour] = (
            left[first] * right[second]
            - left[3 + first] * right[3 + second]
            - (left[second] * right[first] - left[3 + second] * right[3 + first])
        )
        parts[3 + colour] = (
            left[first] * right[3 + second]
            + left[3 + first] * right[second]
            - (left[second] * right[3 + first] + left[3 + second] * right[first])
        )
    return parts


def elemental_kernel(factor, slot_ref, field_ref, placed_ref, quark_ref, sum_ref, low_ref, pair_ref):
    vectors = field_ref.shape[1]
    step = pl.program_id(0)

    @pl.when(step == 0)
    def _():
        sum_ref[...] = jnp.zeros_like(sum_ref)

    for colour in range(3):
        real_low = field_ref[colour].astype(jnp.bfloat16)
        imag_low = field_ref[3 + colour].astype(jnp.bfloat16)
        real_at = slice(colour * LANES, (colour + 1) * LANES)
        imag_at = slice((3 + colour) * LANES, (4 + colour) * LANES)
        low_ref[:vectors, real_at] = real_low
        low_ref[:vectors, imag_at] = -imag_low
        low_ref[vectors:, real_at] = imag_low
        low_ref[vectors:, imag_at] = real_low

    base = 0
    row_starts = []
    for group in range(vectors // GROUP):
        width = vectors - group * GROUP
        row_starts += [base + at * width - group * GROUP for at in range(GROUP)]

        def one_left(at, carry, group=group, width=width, base=base):
            left = [
                jnp.broadcast_to(
                    field_ref[part, pl.ds(group * GROUP + at, 1), :], (GROUP, LANES)
                )
                for part in range(6)
            ]
            for tile in range(width // GROUP):
                from_row = (group + tile) * GROUP
                right = [field_ref[part, from_row : from_row + GROUP, :] for part in range(6)]
                parts = pair_diquarks(left, right)
                to_row = pl.multiple_of(base + at * width + tile * GROUP, GROUP)
                for part in range(6):
                    quark_ref[pl.ds(to_row, GROUP), part * LANES : (part + 1) * LANES] = parts[
                        part
                    ].astype(jnp.bfloat16)
            return carry

        lax.fori_loop(0, GROUP, one_left, 0)
        base += GROUP * width

    def one_dot(at, carry):
        rows = pl.ds(pl.multiple_of(at * DOT_ROWS, DOT_ROWS), DOT_ROWS)
        sum_ref[rows, :] += lax.dot_general(
            quark_ref[rows, :],
            low_ref[...],
            (((1,), (1,)), ((), ())),
            preferred_element_type=jnp.float32,
        )
        return carry

    lax.fori_loop(0, sum_ref.shape[0] // DOT_ROWS, one_dot, 0)

    @pl.when(step == pl.num_programs(0) - 1)
    def _():
        pair_at = 0
        for left in range(vectors - 1):
            count = vectors - 1 - left
            start = row_starts[left] + left + 1
            pair_ref[pair_at : pair_at + count, :] = sum_ref[start : start + count, :] * factor
            pair_at += count
        placed_ref[...] = jnp.zeros_like(placed_ref)

        def place(block, carry):
            rows = pl.ds(pl.multiple_of(block * PB, PB), PB)
            placed_ref[slot_ref[block]] = pair_ref[rows, :]
            return carry

        lax.fori_loop(0, slot_ref.shape[0], place, 0)


def elemental_sums(field, block_slot, factor, slot_total):
    vectors, sites = field.shape[1:]
    groups = vectors // GROUP
    rows = GROUP * GROUP * (groups * (groups + 1) // 2)
    pairs = block_slot.shape[0] * PB
    return pl.pallas_call(
        functools.partial(elemental_kernel, factor),
        grid=(sites // LANES,),
        in_specs=[
            pl.BlockSpec(memory_space=pltpu.SMEM),
            pl.BlockSpec((6, vectors, LANES), lambda at: (0, 0, at)),
        ],
        out_specs=pl.BlockSpec((slot_total, PB, 2 * vectors), lambda at: (0, 0, 0)),
        out_shape=jax.ShapeDtypeStruct((slot_total, PB, 2 * vectors), jnp.float32),
        scratch_shapes=[
            pltpu.VMEM((rows, 6 * LANES), jnp.bfloat16),
            pltpu.VMEM((rows, 2 * vectors), jnp.float32),
            pltpu.VMEM((2 * vectors, 6 * LANES), jnp.bfloat16),
            pltpu.VMEM((pairs, 2 * vectors), jnp.float32),
        ],
        compiler_params=pltpu.CompilerParams(vmem_limit_bytes=40 << 20),
        name="elemental_sums",
    )(block_slot, field)


PIECES = 4


def scatter_kernel(levels, placed_ref, out_ref, *scratch):
    held = (placed_ref,) + scratch[: levels - 1]
    landed = scratch[levels - 1 : 2 * levels - 1]
    send_sem, recv_sem = scratch[2 * levels - 1 :]
    me = lax.axis_index("brick")
    bits = [lax.rem(me // (1 << level), 2) for level in range(levels)]
    partners = [me + (1 - 2 * bits[level]) * (1 << level) for level in range(levels)]

    barrier = pltpu.get_barrier_semaphore()
    for partner in partners:
        pl.semaphore_signal(
            barrier, inc=1, device_id={"brick": partner}, device_id_type=pl.DeviceIdType.MESH
        )
    pl.semaphore_wait(barrier, levels)

    rows = out_ref.shape[0] // PIECES

    def view(level, piece, bit):
        whole = (slice(None),) * (levels - level - 1)
        return whole + (bit, pl.ds(piece * rows, rows))

    def copy(level, piece):
        whole = (slice(None),) * (levels - level - 1)
        return pltpu.make_async_remote_copy(
            src_ref=held[level].at[view(level, piece, 1 - bits[level])],
            dst_ref=landed[level].at[whole + (pl.ds(piece * rows, rows),)],
            send_sem=send_sem.at[level, piece],
            recv_sem=recv_sem.at[level, piece],
            device_id={"brick": partners[level]},
            device_id_type=pl.DeviceIdType.MESH,
        )

    for piece in range(PIECES):
        copy(0, piece).start()
    for level in range(levels):
        for piece in range(PIECES):
            copy(level, piece).wait_recv()
            whole = (slice(None),) * (levels - level - 1)
            part = whole + (pl.ds(piece * rows, rows),)
            total = held[level][view(level, piece, bits[level])] + landed[level][part]
            if level + 1 < levels:
                held[level + 1][part] = total
                copy(level + 1, piece).start()
            else:
                out_ref[part] = total
    for level in range(levels):
        for piece in range(PIECES):
            copy(level, piece).wait_send()


def scatter_sums(placed):
    devices = lax.axis_size("brick")
    levels = devices.bit_length() - 1
    rows = placed.shape[0] // devices * placed.shape[1]
    width = placed.shape[2]
    shapes = [(2,) * (levels - level) + (rows, width) for level in range(levels + 1)]
    out = pl.pallas_call(
        functools.partial(scatter_kernel, levels),
        in_specs=[pl.BlockSpec(memory_space=pltpu.VMEM)],
        out_specs=pl.BlockSpec(memory_space=pltpu.VMEM),
        out_shape=jax.ShapeDtypeStruct((rows, width), jnp.float32),
        scratch_shapes=[pltpu.VMEM(shape, jnp.float32) for shape in shapes[1:levels]]
        + [pltpu.VMEM(shape, jnp.float32) for shape in shapes[1:]]
        + [pltpu.SemaphoreType.DMA((levels, PIECES)), pltpu.SemaphoreType.DMA((levels, PIECES))],
        compiler_params=pltpu.CompilerParams(
            collective_id=0, has_side_effects=True, vmem_limit_bytes=24 << 20
        ),
        name="scatter_sums",
    )(placed.reshape(shapes[0]))
    return out.reshape(placed.shape[0] // devices, placed.shape[1], width)


def grow_rim(lattice_field):
    return padded(lattice_field, (("brick", 3),), 1)


def on_device(eigen_vectors, link_field, block_slot):
    rim_depth = 1
    plane_total = link_field.shape[4]
    lower_links = from_behind(link_field[:, :, :, :, plane_total - rim_depth :], "brick", 1)
    unused_plane = jnp.zeros_like(link_field[:, :, :, :, :1])
    link_wide = jnp.concatenate([lower_links, link_field, unused_plane], 4)
    first_step = apply_hops(grow_rim(eigen_vectors), link_wide)
    filtered = 2.0 * apply_hops(grow_rim(first_step), link_wide) - eigen_vectors
    brick_count = lax.axis_size("brick")
    vector_count = filtered.shape[0]
    lattice_depth = filtered.shape[3] * brick_count
    factor = 1.0 / math.sqrt(3.0 * LX * LY * lattice_depth)
    field = jnp.transpose(filtered, (1, 2, 0, 3, 4)).reshape(6, vector_count, -1)
    return scatter_sums(elemental_sums(field, block_slot, factor, CAP * brick_count))


def solution(mesh):
    return jax.shard_map(
        on_device,
        mesh=mesh,
        in_specs=(
            P(None, None, None, ("cuts", "brick"), None),
            P(None, None, None, None, ("cuts", "brick"), None),
            P(),
        ),
        out_specs=P(("cuts", "brick"), None, None),
        check_vma=False,
    )
```

```python
import functools
import math

import jax
import jax.numpy as jnp
from jax import lax
from jax.experimental import pallas as pl
from jax.experimental.pallas import tpu as pltpu
from jax.sharding import PartitionSpec as P

PB = 32
CAP = 4
LX = 8
LY = 64


LANES = 128
VECTOR_GROUPS = 4
TILE = 8


def shifted_columns(row, column, forward):
    lanes = row.shape[-1]
    if forward:
        return jnp.where(
            column == LX - 1, pltpu.roll(row, LX - 1, 1), pltpu.roll(row, lanes - 1, 1)
        )
    return jnp.where(column == 0, pltpu.roll(row, lanes - LX + 1, 1), pltpu.roll(row, 1, 1))


def times_link(links, field, adjoint, totals):
    for row in range(3):
        for col in range(3):
            at = col * 3 + row if adjoint else row * 3 + col
            real, imag = links(at), links(9 + at)
            if adjoint:
                terms = (
                    real * field[col] + imag * field[3 + col],
                    real * field[3 + col] - imag * field[col],
                )
            else:
                terms = (
                    real * field[col] - imag * field[3 + col],
                    real * field[3 + col] + imag * field[col],
                )
            for part, term in zip((row, 3 + row), terms):
                totals[part] = term if totals[part] is None else totals[part] + term


def filter_kernel(
    eigen_ref,
    link_ref,
    out_ref,
    first_ref,
    near_halo,
    far_halo,
    lower_ref,
    wide_ref,
    send_sem,
    recv_sem,
    link_send,
    link_recv,
):
    planes, _, vectors, sites = eigen_ref.shape
    count = lax.axis_size("brick")
    me = lax.axis_index("brick")
    above = lax.rem(me + 1, count)
    below = lax.rem(me + count - 1, count)
    group_rows = vectors // VECTOR_GROUPS

    barrier = pltpu.get_barrier_semaphore()
    for other in (below, above):
        pl.semaphore_signal(
            barrier, inc=1, device_id={"brick": other}, device_id_type=pl.DeviceIdType.MESH
        )
    pl.semaphore_wait(barrier, 2)

    def halo_copy(hop, side, group):
        source = (eigen_ref, first_ref)[hop]
        target = (near_halo, far_halo)[hop]
        rows = pl.ds(group * group_rows, group_rows)
        return pltpu.make_async_remote_copy(
            src_ref=source.at[planes - 1 if side == 0 else 0, :, rows],
            dst_ref=target.at[side, :, rows],
            send_sem=send_sem.at[hop, side, group],
            recv_sem=recv_sem.at[hop, side, group],
            device_id={"brick": above if side == 0 else below},
            device_id_type=pl.DeviceIdType.MESH,
        )

    link_copy = pltpu.make_async_remote_copy(
        src_ref=link_ref.at[2, planes - 1],
        dst_ref=lower_ref,
        send_sem=link_send,
        recv_sem=link_recv,
        device_id={"brick": above},
        device_id_type=pl.DeviceIdType.MESH,
    )
    link_copy.start()
    for group in range(VECTOR_GROUPS):
        for side in range(2):
            halo_copy(0, side, group).start()

    def widen(direction, plane, block):
        for at in range(18):
            wide_ref[direction, at, plane] = jnp.broadcast_to(block[at : at + 1], (TILE, sites))

    link_column = lax.broadcasted_iota(jnp.int32, (18, sites), 1) % LX
    for plane in range(planes):
        along_x, along_y, along_z = (link_ref[axis, plane] for axis in range(3))
        widen(0, plane, along_x)
        widen(1, plane, shifted_columns(along_x, link_column, False))
        widen(2, plane, along_y)
        widen(3, plane, pltpu.roll(along_y, LX, 1))
        widen(4, plane, along_z)
        if plane > 0:
            widen(5, plane, link_ref[2, plane - 1])
    link_copy.wait_recv()
    widen(5, 0, lower_ref[...])

    lane = lax.broadcasted_iota(jnp.int32, (TILE, LANES), 1)
    column = lane % LX
    chunks = sites // LANES

    def hop_group(source, halo, group, plane, finish):
        def one_tile(at, carry):
            chunk = lax.rem(at, chunks)
            row = pl.multiple_of(group * group_rows + (at // chunks) * TILE, TILE)
            rows = pl.ds(row, TILE)

            def lanes_of(which):
                return pl.ds(pl.multiple_of(which * LANES, LANES), LANES)

            here = lanes_of(chunk)
            after = lanes_of(lax.rem(chunk + 1, chunks))
            before = lanes_of(lax.rem(chunk + chunks - 1, chunks))
            middle = [source[plane, part, rows, here] for part in range(6)]
            totals = [None] * 6

            def links(direction):
                return lambda at: wide_ref[direction, at, plane, :, here]

            field = [shifted_columns(cell, column, True) for cell in middle]
            times_link(links(0), field, False, totals)
            field = [shifted_columns(cell, column, False) for cell in middle]
            times_link(links(1), field, True, totals)
            field = [
                jnp.where(
                    lane < LANES - LX,
                    pltpu.roll(middle[part], LANES - LX, 1),
                    pltpu.roll(source[plane, part, rows, after], LANES - LX, 1),
                )
                for part in range(6)
            ]
            times_link(links(2), field, False, totals)
            field = [
                jnp.where(
                    lane >= LX,
                    pltpu.roll(middle[part], LX, 1),
                    pltpu.roll(source[plane, part, rows, before], LX, 1),
                )
                for part in range(6)
            ]
            times_link(links(3), field, True, totals)
            if plane + 1 < planes:
                field = [source[plane + 1, part, rows, here] for part in range(6)]
            else:
                field = [halo[1, part, rows, here] for part in range(6)]
            times_link(links(4), field, False, totals)
            if plane > 0:
                field = [source[plane - 1, part, rows, here] for part in range(6)]
            else:
                field = [halo[0, part, rows, here] for part in range(6)]
            times_link(links(5), field, True, totals)
            for part in range(6):
                finish(plane, part, rows, here, totals[part] * (1.0 / 6.0))
            return carry

        lax.fori_loop(0, chunks * (group_rows // TILE), one_tile, 0)

    def keep_first(plane, part, rows, here, value):
        first_ref[plane, part, rows, here] = value

    def keep_filtered(plane, part, rows, here, value):
        out_ref[plane, part, rows, here] = 2.0 * value - eigen_ref[plane, part, rows, here]

    for hop in range(2):
        for group in range(VECTOR_GROUPS):
            for side in range(2):
                halo_copy(hop, side, group).wait_recv()
            for plane in range(planes):
                if hop == 0:
                    hop_group(eigen_ref, near_halo, group, plane, keep_first)
                else:
                    hop_group(first_ref, far_halo, group, plane, keep_filtered)
            if hop == 0:
                for side in range(2):
                    halo_copy(1, side, group).start()
    link_copy.wait_send()
    for hop in range(2):
        for group in range(VECTOR_GROUPS):
            for side in range(2):
                halo_copy(hop, side, group).wait_send()


def filtered_field(eigen, links):
    planes, parts, vectors, sites = eigen.shape
    halo = pltpu.VMEM((2, parts, vectors, sites), jnp.float32)
    vmem = pl.BlockSpec(memory_space=pltpu.VMEM)
    copies = (2, 2, VECTOR_GROUPS)
    return pl.pallas_call(
        filter_kernel,
        in_specs=[vmem, vmem],
        out_specs=vmem,
        out_shape=jax.ShapeDtypeStruct(eigen.shape, jnp.float32),
        scratch_shapes=[
            pltpu.VMEM(eigen.shape, jnp.float32),
            halo,
            halo,
            pltpu.VMEM((18, sites), jnp.float32),
            pltpu.VMEM((6, 18, planes, TILE, sites), jnp.float32),
            pltpu.SemaphoreType.DMA(copies),
            pltpu.SemaphoreType.DMA(copies),
            pltpu.SemaphoreType.DMA,
            pltpu.SemaphoreType.DMA,
        ],
        compiler_params=pltpu.CompilerParams(
            collective_id=1, has_side_effects=True, vmem_limit_bytes=24 << 20
        ),
        name="filtered_field",
    )(eigen, links)


GROUP = 16
DOT_ROWS = 256


def pair_diquarks(left, right):
    parts = [None] * 6
    for colour in range(3):
        first = (colour + 1) % 3
        second = (colour + 2) % 3
        parts[colour] = (
            left[first] * right[second]
            - left[3 + first] * right[3 + second]
            - (left[second] * right[first] - left[3 + second] * right[3 + first])
        )
        parts[3 + colour] = (
            left[first] * right[3 + second]
            + left[3 + first] * right[second]
            - (left[second] * right[3 + first] + left[3 + second] * right[first])
        )
    return parts


def elemental_kernel(factor, slot_ref, field_ref, placed_ref, quark_ref, sum_ref, low_ref, pair_ref):
    vectors = field_ref.shape[1]
    step = pl.program_id(0)

    @pl.when(step == 0)
    def _():
        sum_ref[...] = jnp.zeros_like(sum_ref)

    for colour in range(3):
        real_low = field_ref[colour].astype(jnp.bfloat16)
        imag_low = field_ref[3 + colour].astype(jnp.bfloat16)
        real_at = slice(colour * LANES, (colour + 1) * LANES)
        imag_at = slice((3 + colour) * LANES, (4 + colour) * LANES)
        low_ref[:vectors, real_at] = real_low
        low_ref[:vectors, imag_at] = -imag_low
        low_ref[vectors:, real_at] = imag_low
        low_ref[vectors:, imag_at] = real_low

    base = 0
    row_starts = []
    for group in range(vectors // GROUP):
        width = vectors - group * GROUP
        row_starts += [base + at * width - group * GROUP for at in range(GROUP)]

        def one_left(at, carry, group=group, width=width, base=base):
            left = [
                jnp.broadcast_to(
                    field_ref[part, pl.ds(group * GROUP + at, 1), :], (GROUP, LANES)
                )
                for part in range(6)
            ]
            for tile in range(width // GROUP):
                from_row = (group + tile) * GROUP
                right = [field_ref[part, from_row : from_row + GROUP, :] for part in range(6)]
                parts = pair_diquarks(left, right)
                to_row = pl.multiple_of(base + at * width + tile * GROUP, GROUP)
                for part in range(6):
                    quark_ref[pl.ds(to_row, GROUP), part * LANES : (part + 1) * LANES] = parts[
                        part
                    ].astype(jnp.bfloat16)
            return carry

        lax.fori_loop(0, GROUP, one_left, 0)
        base += GROUP * width

    def one_dot(at, carry):
        rows = pl.ds(pl.multiple_of(at * DOT_ROWS, DOT_ROWS), DOT_ROWS)
        sum_ref[rows, :] += lax.dot_general(
            quark_ref[rows, :],
            low_ref[...],
            (((1,), (1,)), ((), ())),
            preferred_element_type=jnp.float32,
        )
        return carry

    lax.fori_loop(0, sum_ref.shape[0] // DOT_ROWS, one_dot, 0)

    @pl.when(step == pl.num_programs(0) - 1)
    def _():
        pair_at = 0
        for left in range(vectors - 1):
            count = vectors - 1 - left
            start = row_starts[left] + left + 1
            pair_ref[pair_at : pair_at + count, :] = sum_ref[start : start + count, :] * factor
            pair_at += count
        placed_ref[...] = jnp.zeros_like(placed_ref)

        def place(block, carry):
            rows = pl.ds(pl.multiple_of(block * PB, PB), PB)
            placed_ref[slot_ref[block]] = pair_ref[rows, :]
            return carry

        lax.fori_loop(0, slot_ref.shape[0], place, 0)


def elemental_sums(field, block_slot, factor, slot_total):
    planes, _, vectors, sites = field.shape
    chunks = sites // LANES
    groups = vectors // GROUP
    rows = GROUP * GROUP * (groups * (groups + 1) // 2)
    pairs = block_slot.shape[0] * PB
    return pl.pallas_call(
        functools.partial(elemental_kernel, factor),
        grid=(planes * chunks,),
        in_specs=[
            pl.BlockSpec(memory_space=pltpu.SMEM),
            pl.BlockSpec(
                (None, 6, vectors, LANES), lambda at: (at // chunks, 0, 0, at % chunks)
            ),
        ],
        out_specs=pl.BlockSpec((slot_total, PB, 2 * vectors), lambda at: (0, 0, 0)),
        out_shape=jax.ShapeDtypeStruct((slot_total, PB, 2 * vectors), jnp.float32),
        scratch_shapes=[
            pltpu.VMEM((rows, 6 * LANES), jnp.bfloat16),
            pltpu.VMEM((rows, 2 * vectors), jnp.float32),
            pltpu.VMEM((2 * vectors, 6 * LANES), jnp.bfloat16),
            pltpu.VMEM((pairs, 2 * vectors), jnp.float32),
        ],
        compiler_params=pltpu.CompilerParams(vmem_limit_bytes=40 << 20),
        name="elemental_sums",
    )(block_slot, field)


PIECES = 4


def scatter_kernel(levels, placed_ref, out_ref, *scratch):
    held = (placed_ref,) + scratch[: levels - 1]
    landed = scratch[levels - 1 : 2 * levels - 1]
    send_sem, recv_sem = scratch[2 * levels - 1 :]
    me = lax.axis_index("brick")
    bits = [lax.rem(me // (1 << level), 2) for level in range(levels)]
    partners = [me + (1 - 2 * bits[level]) * (1 << level) for level in range(levels)]

    barrier = pltpu.get_barrier_semaphore()
    for partner in partners:
        pl.semaphore_signal(
            barrier, inc=1, device_id={"brick": partner}, device_id_type=pl.DeviceIdType.MESH
        )
    pl.semaphore_wait(barrier, levels)

    rows = out_ref.shape[0] // PIECES

    def view(level, piece, bit):
        whole = (slice(None),) * (levels - level - 1)
        return whole + (bit, pl.ds(piece * rows, rows))

    def copy(level, piece):
        whole = (slice(None),) * (levels - level - 1)
        return pltpu.make_async_remote_copy(
            src_ref=held[level].at[view(level, piece, 1 - bits[level])],
            dst_ref=landed[level].at[whole + (pl.ds(piece * rows, rows),)],
            send_sem=send_sem.at[level, piece],
            recv_sem=recv_sem.at[level, piece],
            device_id={"brick": partners[level]},
            device_id_type=pl.DeviceIdType.MESH,
        )

    for piece in range(PIECES):
        copy(0, piece).start()
    for level in range(levels):
        for piece in range(PIECES):
            copy(level, piece).wait_recv()
            whole = (slice(None),) * (levels - level - 1)
            part = whole + (pl.ds(piece * rows, rows),)
            total = held[level][view(level, piece, bits[level])] + landed[level][part]
            if level + 1 < levels:
                held[level + 1][part] = total
                copy(level + 1, piece).start()
            else:
                out_ref[part] = total
    for level in range(levels):
        for piece in range(PIECES):
            copy(level, piece).wait_send()


def scatter_sums(placed):
    devices = lax.axis_size("brick")
    levels = devices.bit_length() - 1
    rows = placed.shape[0] // devices * placed.shape[1]
    width = placed.shape[2]
    shapes = [(2,) * (levels - level) + (rows, width) for level in range(levels + 1)]
    out = pl.pallas_call(
        functools.partial(scatter_kernel, levels),
        in_specs=[pl.BlockSpec(memory_space=pltpu.VMEM)],
        out_specs=pl.BlockSpec(memory_space=pltpu.VMEM),
        out_shape=jax.ShapeDtypeStruct((rows, width), jnp.float32),
        scratch_shapes=[pltpu.VMEM(shape, jnp.float32) for shape in shapes[1:levels]]
        + [pltpu.VMEM(shape, jnp.float32) for shape in shapes[1:]]
        + [pltpu.SemaphoreType.DMA((levels, PIECES)), pltpu.SemaphoreType.DMA((levels, PIECES))],
        compiler_params=pltpu.CompilerParams(
            collective_id=0, has_side_effects=True, vmem_limit_bytes=24 << 20
        ),
        name="scatter_sums",
    )(placed.reshape(shapes[0]))
    return out.reshape(placed.shape[0] // devices, placed.shape[1], width)


def on_device(eigen_vectors, link_field, block_slot):
    vector_count = eigen_vectors.shape[0]
    planes, sites = eigen_vectors.shape[3:]
    eigen = jnp.transpose(eigen_vectors, (3, 1, 2, 0, 4)).reshape(planes, 6, vector_count, sites)
    links = jnp.transpose(link_field, (0, 4, 1, 2, 3, 5)).reshape(3, planes, 18, sites)
    brick_count = lax.axis_size("brick")
    factor = 1.0 / math.sqrt(3.0 * LX * LY * planes * brick_count)
    field = filtered_field(eigen, links)
    return scatter_sums(elemental_sums(field, block_slot, factor, CAP * brick_count))


def solution(mesh):
    return jax.shard_map(
        on_device,
        mesh=mesh,
        in_specs=(
            P(None, None, None, ("cuts", "brick"), None),
            P(None, None, None, None, ("cuts", "brick"), None),
            P(),
        ),
        out_specs=P(("cuts", "brick"), None, None),
        check_vma=False,
    )
```

```python
import functools
import math

import jax
import jax.numpy as jnp
from jax import lax
from jax.experimental import pallas as pl
from jax.experimental.pallas import tpu as pltpu
from jax.sharding import PartitionSpec as P

PB = 32
CAP = 4
LX = 8
LY = 64


LANES = 128
VECTOR_GROUPS = 4
TILE = 8


def shifted_columns(row, column, forward):
    lanes = row.shape[-1]
    if forward:
        return jnp.where(
            column == LX - 1, pltpu.roll(row, LX - 1, 1), pltpu.roll(row, lanes - 1, 1)
        )
    return jnp.where(column == 0, pltpu.roll(row, lanes - LX + 1, 1), pltpu.roll(row, 1, 1))


def times_link(links, field, adjoint, totals):
    for row in range(3):
        for col in range(3):
            at = col * 3 + row if adjoint else row * 3 + col
            real, imag = links(at), links(9 + at)
            if adjoint:
                terms = (
                    real * field[col] + imag * field[3 + col],
                    real * field[3 + col] - imag * field[col],
                )
            else:
                terms = (
                    real * field[col] - imag * field[3 + col],
                    real * field[3 + col] + imag * field[col],
                )
            for part, term in zip((row, 3 + row), terms):
                totals[part] = term if totals[part] is None else totals[part] + term


def filter_kernel(
    eigen_ref,
    link_ref,
    out_ref,
    first_ref,
    near_halo,
    far_halo,
    lower_ref,
    wide_ref,
    send_sem,
    recv_sem,
    link_send,
    link_recv,
):
    planes, _, vectors, sites = eigen_ref.shape
    count = lax.axis_size("brick")
    me = lax.axis_index("brick")
    above = lax.rem(me + 1, count)
    below = lax.rem(me + count - 1, count)
    group_rows = vectors // VECTOR_GROUPS

    barrier = pltpu.get_barrier_semaphore()
    for other in (below, above):
        pl.semaphore_signal(
            barrier, inc=1, device_id={"brick": other}, device_id_type=pl.DeviceIdType.MESH
        )
    pl.semaphore_wait(barrier, 2)

    def halo_copy(hop, side, group):
        source = (eigen_ref, first_ref)[hop]
        target = (near_halo, far_halo)[hop]
        rows = pl.ds(group * group_rows, group_rows)
        return pltpu.make_async_remote_copy(
            src_ref=source.at[planes - 1 if side == 0 else 0, :, rows],
            dst_ref=target.at[side, :, rows],
            send_sem=send_sem.at[hop, side, group],
            recv_sem=recv_sem.at[hop, side, group],
            device_id={"brick": above if side == 0 else below},
            device_id_type=pl.DeviceIdType.MESH,
        )

    link_copy = pltpu.make_async_remote_copy(
        src_ref=link_ref.at[2, planes - 1],
        dst_ref=lower_ref,
        send_sem=link_send,
        recv_sem=link_recv,
        device_id={"brick": above},
        device_id_type=pl.DeviceIdType.MESH,
    )
    link_copy.start()
    for group in range(VECTOR_GROUPS):
        for side in range(2):
            halo_copy(0, side, group).start()

    def widen(direction, plane, block):
        for at in range(18):
            wide_ref[direction, at, plane] = jnp.broadcast_to(block[at : at + 1], (TILE, sites))

    link_column = lax.broadcasted_iota(jnp.int32, (18, sites), 1) % LX
    for plane in range(planes):
        along_x, along_y, along_z = (link_ref[axis, plane] for axis in range(3))
        widen(0, plane, along_x)
        widen(1, plane, shifted_columns(along_x, link_column, False))
        widen(2, plane, along_y)
        widen(3, plane, pltpu.roll(along_y, LX, 1))
        widen(4, plane, along_z)
        if plane > 0:
            widen(5, plane, link_ref[2, plane - 1])
    link_copy.wait_recv()
    widen(5, 0, lower_ref[...])

    lane = lax.broadcasted_iota(jnp.int32, (TILE, LANES), 1)
    column = lane % LX
    chunks = sites // LANES

    def hop_group(source, halo, group, plane, finish):
        def one_tile(at, carry):
            chunk = lax.rem(at, chunks)
            row = pl.multiple_of(group * group_rows + (at // chunks) * TILE, TILE)
            rows = pl.ds(row, TILE)

            def lanes_of(which):
                return pl.ds(pl.multiple_of(which * LANES, LANES), LANES)

            here = lanes_of(chunk)
            after = lanes_of(lax.rem(chunk + 1, chunks))
            before = lanes_of(lax.rem(chunk + chunks - 1, chunks))
            middle = [source[plane, part, rows, here] for part in range(6)]
            totals = [None] * 6

            def links(direction):
                return lambda at: wide_ref[direction, at, plane, :, here]

            field = [shifted_columns(cell, column, True) for cell in middle]
            times_link(links(0), field, False, totals)
            field = [shifted_columns(cell, column, False) for cell in middle]
            times_link(links(1), field, True, totals)
            field = [
                jnp.where(
                    lane < LANES - LX,
                    pltpu.roll(middle[part], LANES - LX, 1),
                    pltpu.roll(source[plane, part, rows, after], LANES - LX, 1),
                )
                for part in range(6)
            ]
            times_link(links(2), field, False, totals)
            field = [
                jnp.where(
                    lane >= LX,
                    pltpu.roll(middle[part], LX, 1),
                    pltpu.roll(source[plane, part, rows, before], LX, 1),
                )
                for part in range(6)
            ]
            times_link(links(3), field, True, totals)
            if plane + 1 < planes:
                field = [source[plane + 1, part, rows, here] for part in range(6)]
            else:
                field = [halo[1, part, rows, here] for part in range(6)]
            times_link(links(4), field, False, totals)
            if plane > 0:
                field = [source[plane - 1, part, rows, here] for part in range(6)]
            else:
                field = [halo[0, part, rows, here] for part in range(6)]
            times_link(links(5), field, True, totals)
            for part in range(6):
                finish(plane, part, rows, here, totals[part] * (1.0 / 6.0))
            return carry

        lax.fori_loop(0, chunks * (group_rows // TILE), one_tile, 0)

    def keep_first(plane, part, rows, here, value):
        first_ref[plane, part, rows, here] = value

    def keep_filtered(plane, part, rows, here, value):
        out_ref[plane, part, rows, here] = 2.0 * value - eigen_ref[plane, part, rows, here]

    for hop in range(2):
        for group in range(VECTOR_GROUPS):
            for side in range(2):
                halo_copy(hop, side, group).wait_recv()
            for plane in range(planes):
                if hop == 0:
                    hop_group(eigen_ref, near_halo, group, plane, keep_first)
                else:
                    hop_group(first_ref, far_halo, group, plane, keep_filtered)
            if hop == 0:
                for side in range(2):
                    halo_copy(1, side, group).start()
    link_copy.wait_send()
    for hop in range(2):
        for group in range(VECTOR_GROUPS):
            for side in range(2):
                halo_copy(hop, side, group).wait_send()


def filtered_field(eigen, links):
    planes, parts, vectors, sites = eigen.shape
    halo = pltpu.VMEM((2, parts, vectors, sites), jnp.float32)
    vmem = pl.BlockSpec(memory_space=pltpu.VMEM)
    copies = (2, 2, VECTOR_GROUPS)
    return pl.pallas_call(
        filter_kernel,
        in_specs=[vmem, vmem],
        out_specs=vmem,
        out_shape=jax.ShapeDtypeStruct(eigen.shape, jnp.float32),
        scratch_shapes=[
            pltpu.VMEM(eigen.shape, jnp.float32),
            halo,
            halo,
            pltpu.VMEM((18, sites), jnp.float32),
            pltpu.VMEM((6, 18, planes, TILE, sites), jnp.float32),
            pltpu.SemaphoreType.DMA(copies),
            pltpu.SemaphoreType.DMA(copies),
            pltpu.SemaphoreType.DMA,
            pltpu.SemaphoreType.DMA,
        ],
        compiler_params=pltpu.CompilerParams(
            collective_id=1, has_side_effects=True, vmem_limit_bytes=24 << 20
        ),
        name="filtered_field",
    )(eigen, links)


ROW_TILE = 8
DOT_TILES = 40


def pair_diquarks(left, right):
    parts = [None] * 6
    for colour in range(3):
        first = (colour + 1) % 3
        second = (colour + 2) % 3
        common = left[6 + first] * right[second] - left[6 + second] * right[first]
        turned = left[first] * right[3 + second] - left[second] * right[3 + first]
        summed = left[3 + first] * right[6 + second] - left[3 + second] * right[6 + first]
        parts[colour] = common - summed
        parts[3 + colour] = common + turned
    return parts


def row_tiles(vectors):
    tiles = []
    row_starts = []
    for left in range(vectors - 1):
        lowest = (left + 1) // ROW_TILE
        row_starts.append((len(tiles) - lowest) * ROW_TILE)
        tiles += [(left, tile) for tile in range(lowest, vectors // ROW_TILE)]
    return tiles, row_starts


def elemental_kernel(
    factor, slot_ref, field_ref, placed_ref, quark_ref, sum_ref, low_ref, pair_ref, mixed_ref
):
    vectors = field_ref.shape[1]
    step = pl.program_id(0)

    @pl.when(step == 0)
    def _():
        sum_ref[...] = jnp.zeros_like(sum_ref)

    for colour in range(3):
        real = field_ref[colour]
        imag = field_ref[3 + colour]
        mixed_ref[colour] = imag - real
        mixed_ref[3 + colour] = imag + real
        real_low = real.astype(jnp.bfloat16)
        imag_low = imag.astype(jnp.bfloat16)
        real_at = slice(colour * LANES, (colour + 1) * LANES)
        imag_at = slice((3 + colour) * LANES, (4 + colour) * LANES)
        low_ref[:vectors, real_at] = real_low
        low_ref[:vectors, imag_at] = -imag_low
        low_ref[vectors:, real_at] = imag_low
        low_ref[vectors:, imag_at] = real_low

    tiles, row_starts = row_tiles(vectors)

    def one_tile(left_at, tile):
        rows = slice(tile * ROW_TILE, (tile + 1) * ROW_TILE)

        def spread(ref, part):
            return jnp.broadcast_to(ref[part, left_at : left_at + 1, :], (ROW_TILE, LANES))

        left = [spread(field_ref, part) for part in range(6)]
        left += [spread(mixed_ref, 3 + colour) for colour in range(3)]
        right = [field_ref[colour, rows, :] for colour in range(3)]
        right += [mixed_ref[part, rows, :] for part in range(6)]
        return pair_diquarks(left, right)

    for from_tile in range(0, len(tiles), DOT_TILES):
        to_tile = min(from_tile + DOT_TILES, len(tiles))
        for at in range(from_tile, to_tile, 2):
            upper = one_tile(*tiles[at])
            lower = one_tile(*tiles[at + 1])
            for part in range(6):
                quark_ref[
                    at * ROW_TILE : (at + 2) * ROW_TILE, part * LANES : (part + 1) * LANES
                ] = jnp.concatenate([upper[part], lower[part]], 0).astype(jnp.bfloat16)
        rows = slice(from_tile * ROW_TILE, to_tile * ROW_TILE)
        sum_ref[rows, :] += lax.dot_general(
            quark_ref[rows, :],
            low_ref[...],
            (((1,), (1,)), ((), ())),
            preferred_element_type=jnp.float32,
        )

    @pl.when(step == pl.num_programs(0) - 1)
    def _():
        pair_at = 0
        for left in range(vectors - 1):
            count = vectors - 1 - left
            start = row_starts[left] + left + 1
            pair_ref[pair_at : pair_at + count, :] = sum_ref[start : start + count, :] * factor
            pair_at += count
        placed_ref[...] = jnp.zeros_like(placed_ref)

        def place(block, carry):
            rows = pl.ds(pl.multiple_of(block * PB, PB), PB)
            placed_ref[slot_ref[block]] = pair_ref[rows, :]
            return carry

        lax.fori_loop(0, slot_ref.shape[0], place, 0)


def elemental_sums(field, block_slot, factor, slot_total):
    planes, _, vectors, sites = field.shape
    chunks = sites // LANES
    rows = len(row_tiles(vectors)[0]) * ROW_TILE
    pairs = block_slot.shape[0] * PB
    return pl.pallas_call(
        functools.partial(elemental_kernel, factor),
        grid=(planes * chunks,),
        in_specs=[
            pl.BlockSpec(memory_space=pltpu.SMEM),
            pl.BlockSpec(
                (None, 6, vectors, LANES), lambda at: (at // chunks, 0, 0, at % chunks)
            ),
        ],
        out_specs=pl.BlockSpec((slot_total, PB, 2 * vectors), lambda at: (0, 0, 0)),
        out_shape=jax.ShapeDtypeStruct((slot_total, PB, 2 * vectors), jnp.float32),
        scratch_shapes=[
            pltpu.VMEM((rows, 6 * LANES), jnp.bfloat16),
            pltpu.VMEM((rows, 2 * vectors), jnp.float32),
            pltpu.VMEM((2 * vectors, 6 * LANES), jnp.bfloat16),
            pltpu.VMEM((pairs, 2 * vectors), jnp.float32),
            pltpu.VMEM((6, vectors, LANES), jnp.float32),
        ],
        compiler_params=pltpu.CompilerParams(vmem_limit_bytes=40 << 20),
        name="elemental_sums",
    )(block_slot, field)


PIECES = 4


def scatter_kernel(levels, placed_ref, out_ref, *scratch):
    held = (placed_ref,) + scratch[: levels - 1]
    landed = scratch[levels - 1 : 2 * levels - 1]
    send_sem, recv_sem = scratch[2 * levels - 1 :]
    me = lax.axis_index("brick")
    bits = [lax.rem(me // (1 << level), 2) for level in range(levels)]
    partners = [me + (1 - 2 * bits[level]) * (1 << level) for level in range(levels)]

    barrier = pltpu.get_barrier_semaphore()
    for partner in partners:
        pl.semaphore_signal(
            barrier, inc=1, device_id={"brick": partner}, device_id_type=pl.DeviceIdType.MESH
        )
    pl.semaphore_wait(barrier, levels)

    rows = out_ref.shape[0] // PIECES

    def view(level, piece, bit):
        whole = (slice(None),) * (levels - level - 1)
        return whole + (bit, pl.ds(piece * rows, rows))

    def copy(level, piece):
        whole = (slice(None),) * (levels - level - 1)
        return pltpu.make_async_remote_copy(
            src_ref=held[level].at[view(level, piece, 1 - bits[level])],
            dst_ref=landed[level].at[whole + (pl.ds(piece * rows, rows),)],
            send_sem=send_sem.at[level, piece],
            recv_sem=recv_sem.at[level, piece],
            device_id={"brick": partners[level]},
            device_id_type=pl.DeviceIdType.MESH,
        )

    for piece in range(PIECES):
        copy(0, piece).start()
    for level in range(levels):
        for piece in range(PIECES):
            copy(level, piece).wait_recv()
            whole = (slice(None),) * (levels - level - 1)
            part = whole + (pl.ds(piece * rows, rows),)
            total = held[level][view(level, piece, bits[level])] + landed[level][part]
            if level + 1 < levels:
                held[level + 1][part] = total
                copy(level + 1, piece).start()
            else:
                out_ref[part] = total
    for level in range(levels):
        for piece in range(PIECES):
            copy(level, piece).wait_send()


def scatter_sums(placed):
    devices = lax.axis_size("brick")
    levels = devices.bit_length() - 1
    rows = placed.shape[0] // devices * placed.shape[1]
    width = placed.shape[2]
    shapes = [(2,) * (levels - level) + (rows, width) for level in range(levels + 1)]
    out = pl.pallas_call(
        functools.partial(scatter_kernel, levels),
        in_specs=[pl.BlockSpec(memory_space=pltpu.VMEM)],
        out_specs=pl.BlockSpec(memory_space=pltpu.VMEM),
        out_shape=jax.ShapeDtypeStruct((rows, width), jnp.float32),
        scratch_shapes=[pltpu.VMEM(shape, jnp.float32) for shape in shapes[1:levels]]
        + [pltpu.VMEM(shape, jnp.float32) for shape in shapes[1:]]
        + [pltpu.SemaphoreType.DMA((levels, PIECES)), pltpu.SemaphoreType.DMA((levels, PIECES))],
        compiler_params=pltpu.CompilerParams(
            collective_id=0, has_side_effects=True, vmem_limit_bytes=24 << 20
        ),
        name="scatter_sums",
    )(placed.reshape(shapes[0]))
    return out.reshape(placed.shape[0] // devices, placed.shape[1], width)


def on_device(eigen_vectors, link_field, block_slot):
    vector_count = eigen_vectors.shape[0]
    planes, sites = eigen_vectors.shape[3:]
    eigen = jnp.transpose(eigen_vectors, (3, 1, 2, 0, 4)).reshape(planes, 6, vector_count, sites)
    links = jnp.transpose(link_field, (0, 4, 1, 2, 3, 5)).reshape(3, planes, 18, sites)
    brick_count = lax.axis_size("brick")
    factor = 1.0 / math.sqrt(3.0 * LX * LY * planes * brick_count)
    field = filtered_field(eigen, links)
    return scatter_sums(elemental_sums(field, block_slot, factor, CAP * brick_count))


def solution(mesh):
    return jax.shard_map(
        on_device,
        mesh=mesh,
        in_specs=(
            P(None, None, None, ("cuts", "brick"), None),
            P(None, None, None, None, ("cuts", "brick"), None),
            P(),
        ),
        out_specs=P(("cuts", "brick"), None, None),
        check_vma=False,
    )
```

```python
import functools
import math

import jax
import jax.numpy as jnp
from jax import lax
from jax.experimental import pallas as pl
from jax.experimental.pallas import tpu as pltpu
from jax.sharding import PartitionSpec as P

PB = 32
CAP = 4
LX = 8
LY = 64


LANES = 128
VECTOR_GROUPS = 8
TILE = 8


def shifted_columns(row, column, forward):
    lanes = row.shape[-1]
    if forward:
        return jnp.where(
            column == LX - 1, pltpu.roll(row, LX - 1, 1), pltpu.roll(row, lanes - 1, 1)
        )
    return jnp.where(column == 0, pltpu.roll(row, lanes - LX + 1, 1), pltpu.roll(row, 1, 1))


def times_link(links, field, adjoint, totals):
    for row in range(3):
        for col in range(3):
            at = col * 3 + row if adjoint else row * 3 + col
            real, imag = links(at), links(9 + at)
            if adjoint:
                terms = (
                    real * field[col] + imag * field[3 + col],
                    real * field[3 + col] - imag * field[col],
                )
            else:
                terms = (
                    real * field[col] - imag * field[3 + col],
                    real * field[3 + col] + imag * field[col],
                )
            for part, term in zip((row, 3 + row), terms):
                totals[part] = term if totals[part] is None else totals[part] + term


def filter_kernel(
    eigen_ref,
    link_ref,
    out_ref,
    first_ref,
    near_halo,
    far_halo,
    lower_ref,
    wide_ref,
    send_sem,
    recv_sem,
    link_send,
    link_recv,
):
    planes, _, vectors, sites = eigen_ref.shape
    count = lax.axis_size("brick")
    me = lax.axis_index("brick")
    above = lax.rem(me + 1, count)
    below = lax.rem(me + count - 1, count)
    group_rows = vectors // VECTOR_GROUPS

    barrier = pltpu.get_barrier_semaphore()
    for other in (below, above):
        pl.semaphore_signal(
            barrier, inc=1, device_id={"brick": other}, device_id_type=pl.DeviceIdType.MESH
        )
    pl.semaphore_wait(barrier, 2)

    def halo_copy(hop, side, group):
        source = (eigen_ref, first_ref)[hop]
        target = (near_halo, far_halo)[hop]
        rows = pl.ds(group * group_rows, group_rows)
        return pltpu.make_async_remote_copy(
            src_ref=source.at[planes - 1 if side == 0 else 0, :, rows],
            dst_ref=target.at[side, :, rows],
            send_sem=send_sem.at[hop, side, group],
            recv_sem=recv_sem.at[hop, side, group],
            device_id={"brick": above if side == 0 else below},
            device_id_type=pl.DeviceIdType.MESH,
        )

    link_copy = pltpu.make_async_remote_copy(
        src_ref=link_ref.at[2, planes - 1],
        dst_ref=lower_ref,
        send_sem=link_send,
        recv_sem=link_recv,
        device_id={"brick": above},
        device_id_type=pl.DeviceIdType.MESH,
    )
    link_copy.start()
    for group in range(VECTOR_GROUPS):
        for side in range(2):
            halo_copy(0, side, group).start()

    def widen(direction, plane, block):
        for at in range(18):
            wide_ref[direction, at, plane] = jnp.broadcast_to(block[at : at + 1], (TILE, sites))

    link_column = lax.broadcasted_iota(jnp.int32, (18, sites), 1) % LX
    for plane in range(planes):
        along_x, along_y, along_z = (link_ref[axis, plane] for axis in range(3))
        widen(0, plane, along_x)
        widen(1, plane, shifted_columns(along_x, link_column, False))
        widen(2, plane, along_y)
        widen(3, plane, pltpu.roll(along_y, LX, 1))
        widen(4, plane, along_z)
        if plane > 0:
            widen(5, plane, link_ref[2, plane - 1])
    link_copy.wait_recv()
    widen(5, 0, lower_ref[...])

    lane = lax.broadcasted_iota(jnp.int32, (TILE, LANES), 1)
    column = lane % LX
    chunks = sites // LANES

    def hop_group(source, halo, group, plane, finish):
        def one_tile(at, carry):
            chunk = lax.rem(at, chunks)
            row = pl.multiple_of(group * group_rows + (at // chunks) * TILE, TILE)
            rows = pl.ds(row, TILE)

            def lanes_of(which):
                return pl.ds(pl.multiple_of(which * LANES, LANES), LANES)

            here = lanes_of(chunk)
            after = lanes_of(lax.rem(chunk + 1, chunks))
            before = lanes_of(lax.rem(chunk + chunks - 1, chunks))
            middle = [source[plane, part, rows, here] for part in range(6)]
            totals = [None] * 6

            def links(direction):
                return lambda at: wide_ref[direction, at, plane, :, here]

            field = [shifted_columns(cell, column, True) for cell in middle]
            times_link(links(0), field, False, totals)
            field = [shifted_columns(cell, column, False) for cell in middle]
            times_link(links(1), field, True, totals)
            field = [
                jnp.where(
                    lane < LANES - LX,
                    pltpu.roll(middle[part], LANES - LX, 1),
                    pltpu.roll(source[plane, part, rows, after], LANES - LX, 1),
                )
                for part in range(6)
            ]
            times_link(links(2), field, False, totals)
            field = [
                jnp.where(
                    lane >= LX,
                    pltpu.roll(middle[part], LX, 1),
                    pltpu.roll(source[plane, part, rows, before], LX, 1),
                )
                for part in range(6)
            ]
            times_link(links(3), field, True, totals)
            if plane + 1 < planes:
                field = [source[plane + 1, part, rows, here] for part in range(6)]
            else:
                field = [halo[1, part, rows, here] for part in range(6)]
            times_link(links(4), field, False, totals)
            if plane > 0:
                field = [source[plane - 1, part, rows, here] for part in range(6)]
            else:
                field = [halo[0, part, rows, here] for part in range(6)]
            times_link(links(5), field, True, totals)
            for part in range(6):
                finish(plane, part, rows, here, totals[part] * (1.0 / 6.0))
            return carry

        lax.fori_loop(0, chunks * (group_rows // TILE), one_tile, 0)

    def keep_first(plane, part, rows, here, value):
        first_ref[plane, part, rows, here] = value

    def keep_filtered(plane, part, rows, here, value):
        out_ref[plane, part, rows, here] = 2.0 * value - eigen_ref[plane, part, rows, here]

    for hop in range(2):
        for group in range(VECTOR_GROUPS):
            for side in range(2):
                halo_copy(hop, side, group).wait_recv()
            for plane in range(planes):
                if hop == 0:
                    hop_group(eigen_ref, near_halo, group, plane, keep_first)
                else:
                    hop_group(first_ref, far_halo, group, plane, keep_filtered)
            if hop == 0:
                for side in range(2):
                    halo_copy(1, side, group).start()
    link_copy.wait_send()
    for hop in range(2):
        for group in range(VECTOR_GROUPS):
            for side in range(2):
                halo_copy(hop, side, group).wait_send()


def filtered_field(eigen, links):
    planes, parts, vectors, sites = eigen.shape
    halo = pltpu.VMEM((2, parts, vectors, sites), jnp.float32)
    vmem = pl.BlockSpec(memory_space=pltpu.VMEM)
    copies = (2, 2, VECTOR_GROUPS)
    return pl.pallas_call(
        filter_kernel,
        in_specs=[vmem, vmem],
        out_specs=vmem,
        out_shape=jax.ShapeDtypeStruct(eigen.shape, jnp.float32),
        scratch_shapes=[
            pltpu.VMEM(eigen.shape, jnp.float32),
            halo,
            halo,
            pltpu.VMEM((18, sites), jnp.float32),
            pltpu.VMEM((6, 18, planes, TILE, sites), jnp.float32),
            pltpu.SemaphoreType.DMA(copies),
            pltpu.SemaphoreType.DMA(copies),
            pltpu.SemaphoreType.DMA,
            pltpu.SemaphoreType.DMA,
        ],
        compiler_params=pltpu.CompilerParams(
            collective_id=1, has_side_effects=True, vmem_limit_bytes=24 << 20
        ),
        name="filtered_field",
    )(eigen, links)


ROW_TILE = 8
DOT_TILES = 40


def pair_diquarks(left, right):
    parts = [None] * 6
    for colour in range(3):
        first = (colour + 1) % 3
        second = (colour + 2) % 3
        common = left[6 + first] * right[second] - left[6 + second] * right[first]
        turned = left[first] * right[3 + second] - left[second] * right[3 + first]
        summed = left[3 + first] * right[6 + second] - left[3 + second] * right[6 + first]
        parts[colour] = common - summed
        parts[3 + colour] = common + turned
    return parts


def row_tiles(vectors):
    tiles = []
    row_starts = []
    for left in range(vectors - 1):
        lowest = (left + 1) // ROW_TILE
        row_starts.append((len(tiles) - lowest) * ROW_TILE)
        tiles += [(left, tile) for tile in range(lowest, vectors // ROW_TILE)]
    return tiles, row_starts


def elemental_kernel(
    factor, slot_ref, field_ref, placed_ref, quark_ref, sum_ref, low_ref, pair_ref, mixed_ref
):
    vectors = field_ref.shape[1]
    step = pl.program_id(0)

    @pl.when(step == 0)
    def _():
        sum_ref[...] = jnp.zeros_like(sum_ref)

    for colour in range(3):
        real = field_ref[colour]
        imag = field_ref[3 + colour]
        mixed_ref[colour] = imag - real
        mixed_ref[3 + colour] = imag + real
        real_low = real.astype(jnp.bfloat16)
        imag_low = imag.astype(jnp.bfloat16)
        real_at = slice(colour * LANES, (colour + 1) * LANES)
        imag_at = slice((3 + colour) * LANES, (4 + colour) * LANES)
        low_ref[:vectors, real_at] = real_low
        low_ref[:vectors, imag_at] = -imag_low
        low_ref[vectors:, real_at] = imag_low
        low_ref[vectors:, imag_at] = real_low

    tiles, row_starts = row_tiles(vectors)

    def one_tile(left_at, tile):
        rows = slice(tile * ROW_TILE, (tile + 1) * ROW_TILE)

        def spread(ref, part):
            return jnp.broadcast_to(ref[part, left_at : left_at + 1, :], (ROW_TILE, LANES))

        left = [spread(field_ref, part) for part in range(6)]
        left += [spread(mixed_ref, 3 + colour) for colour in range(3)]
        right = [field_ref[colour, rows, :] for colour in range(3)]
        right += [mixed_ref[part, rows, :] for part in range(6)]
        return pair_diquarks(left, right)

    for from_tile in range(0, len(tiles), DOT_TILES):
        to_tile = min(from_tile + DOT_TILES, len(tiles))
        for at in range(from_tile, to_tile, 2):
            upper = one_tile(*tiles[at])
            lower = one_tile(*tiles[at + 1])
            for part in range(6):
                quark_ref[
                    at * ROW_TILE : (at + 2) * ROW_TILE, part * LANES : (part + 1) * LANES
                ] = jnp.concatenate([upper[part], lower[part]], 0).astype(jnp.bfloat16)
        rows = slice(from_tile * ROW_TILE, to_tile * ROW_TILE)
        sum_ref[rows, :] += lax.dot_general(
            quark_ref[rows, :],
            low_ref[...],
            (((1,), (1,)), ((), ())),
            preferred_element_type=jnp.float32,
        )

    @pl.when(step == pl.num_programs(0) - 1)
    def _():
        pair_at = 0
        for left in range(vectors - 1):
            count = vectors - 1 - left
            start = row_starts[left] + left + 1
            pair_ref[pair_at : pair_at + count, :] = sum_ref[start : start + count, :] * factor
            pair_at += count
        placed_ref[...] = jnp.zeros_like(placed_ref)

        def place(block, carry):
            rows = pl.ds(pl.multiple_of(block * PB, PB), PB)
            placed_ref[slot_ref[block]] = pair_ref[rows, :]
            return carry

        lax.fori_loop(0, slot_ref.shape[0], place, 0)


def elemental_sums(field, block_slot, factor, slot_total):
    planes, _, vectors, sites = field.shape
    chunks = sites // LANES
    rows = len(row_tiles(vectors)[0]) * ROW_TILE
    pairs = block_slot.shape[0] * PB
    return pl.pallas_call(
        functools.partial(elemental_kernel, factor),
        grid=(planes * chunks,),
        in_specs=[
            pl.BlockSpec(memory_space=pltpu.SMEM),
            pl.BlockSpec(
                (None, 6, vectors, LANES), lambda at: (at // chunks, 0, 0, at % chunks)
            ),
        ],
        out_specs=pl.BlockSpec((slot_total, PB, 2 * vectors), lambda at: (0, 0, 0)),
        out_shape=jax.ShapeDtypeStruct((slot_total, PB, 2 * vectors), jnp.float32),
        scratch_shapes=[
            pltpu.VMEM((rows, 6 * LANES), jnp.bfloat16),
            pltpu.VMEM((rows, 2 * vectors), jnp.float32),
            pltpu.VMEM((2 * vectors, 6 * LANES), jnp.bfloat16),
            pltpu.VMEM((pairs, 2 * vectors), jnp.float32),
            pltpu.VMEM((6, vectors, LANES), jnp.float32),
        ],
        compiler_params=pltpu.CompilerParams(vmem_limit_bytes=40 << 20),
        name="elemental_sums",
    )(block_slot, field)


PIECES = 8


def scatter_kernel(levels, placed_ref, out_ref, *scratch):
    held = (placed_ref,) + scratch[: levels - 1]
    landed = scratch[levels - 1 : 2 * levels - 1]
    send_sem, recv_sem = scratch[2 * levels - 1 :]
    me = lax.axis_index("brick")
    bits = [lax.rem(me // (1 << level), 2) for level in range(levels)]
    partners = [me + (1 - 2 * bits[level]) * (1 << level) for level in range(levels)]

    barrier = pltpu.get_barrier_semaphore()
    for partner in partners:
        pl.semaphore_signal(
            barrier, inc=1, device_id={"brick": partner}, device_id_type=pl.DeviceIdType.MESH
        )
    pl.semaphore_wait(barrier, levels)

    rows = out_ref.shape[0] // PIECES

    def view(level, piece, bit):
        whole = (slice(None),) * (levels - level - 1)
        return whole + (bit, pl.ds(piece * rows, rows))

    def copy(level, piece):
        whole = (slice(None),) * (levels - level - 1)
        return pltpu.make_async_remote_copy(
            src_ref=held[level].at[view(level, piece, 1 - bits[level])],
            dst_ref=landed[level].at[whole + (pl.ds(piece * rows, rows),)],
            send_sem=send_sem.at[level, piece],
            recv_sem=recv_sem.at[level, piece],
            device_id={"brick": partners[level]},
            device_id_type=pl.DeviceIdType.MESH,
        )

    for piece in range(PIECES):
        copy(0, piece).start()
    for level in range(levels):
        for piece in range(PIECES):
            copy(level, piece).wait_recv()
            whole = (slice(None),) * (levels - level - 1)
            part = whole + (pl.ds(piece * rows, rows),)
            total = held[level][view(level, piece, bits[level])] + landed[level][part]
            if level + 1 < levels:
                held[level + 1][part] = total
                copy(level + 1, piece).start()
            else:
                out_ref[part] = total
    for level in range(levels):
        for piece in range(PIECES):
            copy(level, piece).wait_send()


def scatter_sums(placed):
    devices = lax.axis_size("brick")
    levels = devices.bit_length() - 1
    rows = placed.shape[0] // devices * placed.shape[1]
    width = placed.shape[2]
    shapes = [(2,) * (levels - level) + (rows, width) for level in range(levels + 1)]
    out = pl.pallas_call(
        functools.partial(scatter_kernel, levels),
        in_specs=[pl.BlockSpec(memory_space=pltpu.VMEM)],
        out_specs=pl.BlockSpec(memory_space=pltpu.VMEM),
        out_shape=jax.ShapeDtypeStruct((rows, width), jnp.float32),
        scratch_shapes=[pltpu.VMEM(shape, jnp.float32) for shape in shapes[1:levels]]
        + [pltpu.VMEM(shape, jnp.float32) for shape in shapes[1:]]
        + [pltpu.SemaphoreType.DMA((levels, PIECES)), pltpu.SemaphoreType.DMA((levels, PIECES))],
        compiler_params=pltpu.CompilerParams(
            collective_id=0, has_side_effects=True, vmem_limit_bytes=24 << 20
        ),
        name="scatter_sums",
    )(placed.reshape(shapes[0]))
    return out.reshape(placed.shape[0] // devices, placed.shape[1], width)


def on_device(eigen_vectors, link_field, block_slot):
    vector_count = eigen_vectors.shape[0]
    planes, sites = eigen_vectors.shape[3:]
    eigen = jnp.transpose(eigen_vectors, (3, 1, 2, 0, 4)).reshape(planes, 6, vector_count, sites)
    links = jnp.transpose(link_field, (0, 4, 1, 2, 3, 5)).reshape(3, planes, 18, sites)
    brick_count = lax.axis_size("brick")
    factor = 1.0 / math.sqrt(3.0 * LX * LY * planes * brick_count)
    field = filtered_field(eigen, links)
    return scatter_sums(elemental_sums(field, block_slot, factor, CAP * brick_count))


def solution(mesh):
    return jax.shard_map(
        on_device,
        mesh=mesh,
        in_specs=(
            P(None, None, None, ("cuts", "brick"), None),
            P(None, None, None, None, ("cuts", "brick"), None),
            P(),
        ),
        out_specs=P(("cuts", "brick"), None, None),
        check_vma=False,
    )
```
